512 devices in a mesh: lat: 16 (over x, z_hi, core), lon: 32 (over y, z_lo).
Axes of the slice: x: 4, y: 4, z: 16 (z_hi: 2, z_lo: 8; z = z_hi * 8 + z_lo), core: 2. Of those that a mesh axis runs over, the one named last changes fastest.
Arguments:
- latent: bfloat16 [256, 512, 641], P('lat', 'lon'), may hold values from -6 to 6
- filters: bfloat16 [9, 256, 9, 33], P(None, 'lat'), may hold values from -0.59765625 to 0.59765625
- widths: int32 [256, 9], P('lat'), may hold values from 0 to 16, as said below
- mix_weight: bfloat16 [9, 641, 512], P(None, None, ('lat', 'lon')), may hold values from -0.078125 to 0.078125
- mix_bias: float32 [512], replicated, may hold values from -3 to 3
Outputs:
- convolved: bfloat16 [256, 512, 512], P('lat', 'lon')
The draws below stay inside these ranges and needn't reach their ends.
Inputs may be any that keep to these rules, and one draw needn't show every extreme that they name: widths grow toward the poles and are at most 16, reached in rows next to a pole.
All inputs are finite; a program needn't handle non-finite values.
Results may differ from the reference program's by a relative error of at most 0.0048.
Values may be sent and summed in bfloat16 or wider, within the bound.
A program may use at most 64 MiB of HBM per device.

```python
import math
import jax
import jax.numpy as jnp
from jax import lax

CHANNELS = 641
OUT_CH = 512
BASES = 9
RADIUS = 4
LON_REACH = 16
LATITUDES = 256
LONGITUDES = 512


def draw_widths(key, part):
    row_indices = jnp.arange(LATITUDES, dtype=jnp.int32)[:, None]
    lat_offsets = jnp.arange(2 * RADIUS + 1, dtype=jnp.int32)[None, :] - RADIUS
    neighbour = row_indices + lat_offsets
    neighbour = jnp.where(neighbour < 0, -neighbour - 1, neighbour)
    neighbour = jnp.where(neighbour >= LATITUDES, 2 * LATITUDES - 1 - neighbour, neighbour)
    polar_gap = jnp.minimum(neighbour, LATITUDES - 1 - neighbour) + 1
    polar_gap = jnp.minimum(polar_gap, max(LATITUDES // 3, 1))
    chord_lengths = jnp.array([math.isqrt(4 * (RADIUS * RADIUS - offset_value * offset_value)) for offset_value in range(-RADIUS, RADIUS + 1)], jnp.int32)
    geometric = chord_lengths[None, :] * LATITUDES // (3 * polar_gap)
    jitter = jax.random.randint(key, (LATITUDES, 2 * RADIUS + 1), 0, 2, dtype=jnp.int32)
    return jnp.minimum(LON_REACH, geometric + jitter).astype(jnp.int32)


def level_of(stream_key, extent, shards, low, high):
    loudness, own = 1.0, jax.random.fold_in(stream_key, 6)
    for dim, blocks in shards:
        heights = jnp.exp(jax.random.uniform(jax.random.fold_in(own, dim), (blocks,), jnp.float32, low / len(shards), high / len(shards)))
        loudness = loudness * jnp.repeat(heights, extent[dim] // blocks).reshape([-1 if axis == dim else 1 for axis in range(len(extent))])
    return loudness


def centred(own_key, extent, spread, limit, split=(), kind=jnp.bfloat16):
    drawn = spread * jax.random.normal(own_key, extent, jnp.float32)
    if split:
        drawn = drawn * level_of(own_key, extent, split, -0.22, 0.18)
    return jnp.clip(drawn, -limit, limit).astype(kind)


def setup_inputs(seed: int = 0) -> dict:
    splits = jax.random.split(jax.random.key(seed), 6)
    return {
        "latent": centred(splits[0], (LATITUDES, LONGITUDES, CHANNELS), 1.0, 6.0, ((0, 16), (1, 32))),
        "filters": centred(splits[1], (BASES, LATITUDES, 2 * RADIUS + 1, 2 * LON_REACH + 1), 0.1, 0.59765625, ((1, 16),)),
        "widths": draw_widths(jax.random.fold_in(splits[5], 71), 0),
        "mix_weight": centred(splits[3], (BASES, CHANNELS, OUT_CH), (BASES * CHANNELS) ** -0.5, 0.078125, ((2, 512),)),
        "mix_bias": centred(splits[4], (OUT_CH,), 0.5, 3.0, (), jnp.float32),
    }


def extend_rows(latent):
    half_turn = LONGITUDES // 2
    upper_rim = jnp.roll(latent[:RADIUS][::-1], -half_turn, axis=1)
    lower_rim = jnp.roll(latent[-RADIUS:][::-1], -half_turn, axis=1)
    return jnp.concatenate([upper_rim, latent, lower_rim], 0)


def reference(latent, filters, widths, mix_weight, mix_bias):
    extended = extend_rows(latent)
    extended = jnp.concatenate([extended[:, -LON_REACH:], extended, extended[:, :LON_REACH]], 1)
    offsets = jnp.arange(2 * LON_REACH + 1, dtype=jnp.int32) - LON_REACH
    inside = jnp.abs(offsets)[None, None, :] <= widths[:, :, None]
    coefficients = jnp.where(inside[None], filters, jnp.zeros((), filters.dtype))
    weight_broadened = mix_weight.astype(jnp.float32)

    def one_row(row_index):
        slab_rows = lax.dynamic_slice_in_dim(extended, row_index, 2 * RADIUS + 1, 0).astype(jnp.float32)
        row_coefficient = lax.dynamic_index_in_dim(coefficients, row_index, 1, keepdims=False).astype(jnp.float32)

        def add_offset(shift_index, running_total):
            window = lax.dynamic_slice_in_dim(slab_rows, shift_index, LONGITUDES, 1)
            factor = lax.dynamic_index_in_dim(row_coefficient, shift_index, 2, keepdims=False)
            return running_total + jnp.einsum("kd,djc->kjc", factor, window, precision=lax.Precision.HIGHEST)

        summed = lax.fori_loop(0, 2 * LON_REACH + 1, add_offset,
                               jnp.zeros((BASES, LONGITUDES, CHANNELS), jnp.float32))
        features = lax.optimization_barrier(summed.astype(jnp.bfloat16)).astype(jnp.float32)
        channel_mixed_output = jnp.einsum("kjc,kco->jo", features, weight_broadened, precision=lax.Precision.HIGHEST) + mix_bias
        return jax.nn.gelu(channel_mixed_output, approximate=False).astype(jnp.bfloat16)

    return lax.map(one_row, jnp.arange(LATITUDES, dtype=jnp.int32))
```

```python
import math

import jax
import jax.numpy as jnp
from jax import lax
from jax.experimental import pallas as pl
from jax.experimental.pallas import tpu as pltpu
from jax.sharding import PartitionSpec as P

RADIUS = 4
REACH = 16
BASES = 9
MAIN = 640
SPAN = 48
MESH = pl.DeviceIdType.MESH
BF = jnp.bfloat16
F32 = jnp.float32

Z1, P1, H1, P2, H2, DD = range(6)


def device_of(x, y, z, core):
    return (x * 4 + (z // 8) * 2 + core, y * 8 + z % 8)


def build_rows(coef_ref, a_ref, pair):
    lane = lax.broadcasted_iota(jnp.int32, (16, 128), 1)
    zero = jnp.zeros((16, 128), F32)
    for s in range(2):
        for k in range(BASES):
            taps = coef_ref[pair * 2 + s, k].astype(F32)
            taps = jnp.pad(taps, ((0, 0), (0, 128 - taps.shape[1])))
            tiles = [None] * 4

            def put(t, part):
                tiles[t] = part if tiles[t] is None else tiles[t] + part

            for d in range(2 * RADIUS + 1):
                first, at = divmod(SPAN * (d + s), 128)
                line = jnp.broadcast_to(taps[d : d + 1], (16, 128))
                line = pltpu.roll(line, at, 1, stride=1, stride_axis=0)
                if at + SPAN > 128:
                    put(first, jnp.where(lane >= at, line, zero))
                    put(first + 1, jnp.where(lane < at, line, zero))
                else:
                    put(first, line)
            rows = pl.ds((s * BASES + k) * 16, 16)
            a_ref[pair, rows, :] = jnp.concatenate(tiles, 1).astype(BF)


def stencil_rows(a_ref, e_ref, f_ref, pair):
    lane = lax.broadcasted_iota(jnp.int32, (16, 128), 1)
    slab = e_ref[pl.ds(pair * 2, 10)].reshape(10 * SPAN, MAIN + 1)
    found = jnp.dot(a_ref[pair][:, : 10 * SPAN], slab, preferred_element_type=F32)
    for s in range(2):
        rows = pl.ds(pl.multiple_of((pair * 2 + s) * 16, 16), 16)
        last = jnp.zeros((16, 128), F32)
        for k in range(BASES):
            part = found[(s * BASES + k) * 16 : (s * BASES + k + 1) * 16]
            f_ref[rows, k * MAIN : (k + 1) * MAIN] = part[:, :MAIN].astype(BF)
            last = jnp.where(lane == k, jnp.broadcast_to(part[:, MAIN:], (16, 128)), last)
        f_ref[rows, BASES * MAIN :] = last.astype(BF)


def body_kernel(
    w_in, latent, coef_ref, bias_ref, out_ref,
    g_ref, e_ref, a_ref, f_ref, wt_ref,
    send, recv, hsend, hrecv, rsend, rrecv, own_sem,
):
    lat, lon = lax.axis_index("lat"), lax.axis_index("lon")
    x, core = lat // 4, lat % 2
    y = lon // 8
    z = ((lat // 2) % 2) * 8 + lon % 8
    xs = ((x + 3) % 4, (x + 1) % 4)
    ys = ((y + 3) % 4, (y + 1) % 4)
    zs = ((z + 15) % 16, (z + 1) % 16)
    to_x = [device_of(v, y, z, core) for v in xs]
    to_y = [device_of(x, v, z, core) for v in ys]
    to_z = [device_of(x, y, v, core) for v in zs]
    sibling = (lat + 1 - 2 * core, lon)
    to_lon = [(lat, (lon + 31) % 32), (lat, (lon + 1) % 32)]
    top, bottom = lat == 0, lat == 15
    opposite = (lon + 16) % 32
    up = (jnp.where(top, 0, lat - 1), jnp.where(top, opposite, lon))
    down = (jnp.where(bottom, 15, lat + 1), jnp.where(bottom, opposite, lon))

    barrier = pltpu.get_barrier_semaphore()
    peers = to_x + to_y + to_z + [sibling] + to_lon + [up, down]
    for peer in peers:
        pl.semaphore_signal(barrier, inc=1, device_id=peer, device_id_type=MESH)
    pl.semaphore_wait(barrier, len(peers))

    def remote(src, dst, s, r, where):
        return pltpu.make_async_remote_copy(
            src_ref=src, dst_ref=dst, send_sem=s, recv_sem=r,
            device_id=where, device_id_type=MESH,
        )

    def column(part, side):
        begin, size = ((RADIUS, 16), (0, RADIUS), (RADIUS + 16, RADIUS))[part]
        src = latent if part == 0 else e_ref.at[pl.ds(begin, size), pl.ds(16, 16), :]
        dst = e_ref.at[pl.ds(begin, size), pl.ds(32 * (1 - side), 16), :]
        return remote(src, dst, hsend.at[part, side], hrecv.at[part, side], to_lon[side])

    def strip(edge, q):
        pole = top if edge == 0 else bottom
        row = jnp.where(pole, 3 - q, 20 + q) if edge == 0 else jnp.where(pole, 23 - q, q)
        slot = jnp.where(pole, edge, 1 - edge)
        return remote(
            latent.at[edge * 12 + q], e_ref.at[row, pl.ds(16, 16), :],
            rsend.at[edge, q], rrecv.at[slot], down if edge else up,
        )

    for q in range(RADIUS):
        strip(0, q).start()
        strip(1, q).start()
    for side in range(2):
        column(0, side).start()

    def block(zb):
        return g_ref.at[x, zb // 8, core, y, zb % 8]

    own_w = pltpu.make_async_copy(w_in, block(z), own_sem.at[0])
    own_w.start()
    own_e = pltpu.make_async_copy(
        latent, e_ref.at[pl.ds(RADIUS, 16), pl.ds(16, 16), :], own_sem.at[1]
    )
    own_e.start()

    def z_copy(zb, b, side, src=None):
        return remote(
            block(zb) if src is None else src, block(zb),
            send.at[Z1, b, 0], recv.at[Z1, b, 0], to_z[side],
        )

    z_copy(z, 2, 0, w_in).start()
    z_copy(z, 1, 1, w_in).start()
    own_w.wait()

    def pieces(i, odd):
        b = 2 * i + odd
        zb = (z + 15 - i) % 16 if odd else (z + i) % 16
        hi, lo = zb // 8, zb % 8
        near, far = (ys, xs) if odd else (xs, ys)
        to_near, to_far = (to_y, to_x) if odd else (to_x, to_y)

        def one(v, rows=None):
            ref = g_ref.at[x, hi, core, v, lo] if odd else g_ref.at[v, hi, core, y, lo]
            return ref if rows is None else ref.at[rows]

        def line(v, part=slice(None)):
            return g_ref.at[v, hi, core, part, lo] if odd else g_ref.at[part, hi, core, v, lo]

        me = (y, x) if odd else (x, y)
        halves = (pl.ds(0, 24), pl.ds(24, 24))
        pairs = (pl.ds(0, 2), pl.ds(2, 2))

        def sem(stage, side):
            return send.at[stage, b, side], recv.at[stage, b, side]

        def copies(stage, side, incoming=False):
            if stage == P1:
                v = near[side] if incoming else me[0]
                return remote(one(v), one(v), *sem(P1, 1 - side if incoming else side), to_near[side])
            if stage == H1:
                far_one = (me[0] + 2) % 4
                s = 1 - side if incoming else side
                v = far_one if incoming else near[1 - side]
                rows = halves[0] if s == 1 else halves[1]
                return remote(one(v, rows), one(v, rows), *sem(H1, s), to_near[side])
            if stage == P2:
                v = far[side] if incoming else me[1]
                return remote(line(v), line(v), *sem(P2, 1 - side if incoming else side), to_far[side])
            far_line = (me[1] + 2) % 4
            s = 1 - side if incoming else side
            v = far_line if incoming else far[1 - side]
            part = pairs[0] if s == 1 else pairs[1]
            return remote(line(v, part), line(v, part), *sem(H2, s), to_far[side])

        def plane():
            src = g_ref.at[:, hi, core, :, lo]
            return remote(src, src, send.at[DD, b, 0], recv.at[DD, b, 0], sibling)

        return b, zb, copies, plane

    def from_sibling(i, odd):
        b = 2 * i + odd
        zb = (z + 15 - i) % 16 if odd else (z + i) % 16
        dst = g_ref.at[:, zb // 8, 1 - core, :, zb % 8]
        return remote(dst, dst, send.at[DD, b, 0], recv.at[DD, b, 0], sibling)

    def step(t, carry):
        @pl.when(t < 8)
        def _():
            for odd in range(2):
                b, zb, copies, _ = pieces(t, odd)

                def arrive():
                    z_copy(zb, b, 0).wait_recv()

                if odd:
                    arrive()
                else:
                    pl.when(t > 0)(arrive)

                @pl.when((t < 7) & (t > 0) if not odd else t < 7)
                def _():
                    z_copy(zb, b + 2, odd).start()

                for side in range(2):
                    copies(P1, side).start()

        @pl.when((t >= 1) & (t < 9))
        def _():
            for odd in range(2):
                _, _, copies, _ = pieces(t - 1, odd)
                for side in range(2):
                    copies(P1, 1 - side, True).wait_recv()
                    copies(H1, side).start()

        @pl.when((t >= 2) & (t < 10))
        def _():
            for odd in range(2):
                _, _, copies, _ = pieces(t - 2, odd)
                for side in range(2):
                    copies(H1, side, True).wait_recv()
                for side in range(2):
                    copies(P2, side).start()

        @pl.when((t >= 3) & (t < 11))
        def _():
            for odd in range(2):
                _, _, copies, _ = pieces(t - 3, odd)
                for side in range(2):
                    copies(P2, 1 - side, True).wait_recv()
                    copies(H2, side).start()

        @pl.when(t >= 4)
        def _():
            for odd in range(2):
                _, _, copies, plane = pieces(t - 4, odd)
                for side in range(2):
                    copies(H2, side, True).wait_recv()
                plane().start()

        @pl.when(t < 8)
        def _():
            build_rows(coef_ref, a_ref, t)

        @pl.when(t == 5)
        def _():
            for part in (1, 2):
                rows = e_ref.at[pl.ds((0, 20)[part - 1], RADIUS), pl.ds(16, 16), :]
                pltpu.make_async_copy(rows, rows, rrecv.at[part - 1]).wait()
                for side in range(2):
                    column(part, side).start()

        return carry

    lax.fori_loop(0, 12, step, 0)

    own_e.wait()
    for part in range(3):
        for side in range(2):
            column(part, side).wait_recv()

    def features(pair, carry):
        stencil_rows(a_ref, e_ref, f_ref, pair)
        return carry

    lax.fori_loop(0, 8, features, 0)

    def wait_planes(i, carry):
        for odd in range(2):
            from_sibling(i, odd).wait_recv()
        return carry

    lax.fori_loop(0, 8, wait_planes, 0)

    def lay(n, carry):
        band, half = n // 2, n % 2
        rows = g_ref[band // 4, (band // 2) % 2, band % 2, pl.ds(half * 2, 2)]
        flat = rows.reshape(16, 48 * 128)
        wt_ref[pl.ds(pl.multiple_of(n * 16, 16), 16), :] = flat[:, : 46 * 128]
        return carry

    lax.fori_loop(0, 32, lay, 0)

    def mix(n, carry):
        cols = pl.ds(pl.multiple_of(n * 256, 256), 256)
        total = lax.dot_general(
            f_ref[...], wt_ref[cols, :], (((1,), (1,)), ((), ())), preferred_element_type=F32
        )
        total = total + bias_ref[:, cols]
        value = 0.5 * total * (1.0 + lax.erf(total * math.sqrt(0.5)))
        out_ref[:, cols] = value.astype(BF)
        return carry

    lax.fori_loop(0, 2, mix, 0)

    def drain(i, carry):
        for odd in range(2):
            b, zb, copies, plane = pieces(i, odd)

            @pl.when((i > 0) if not odd else (i >= 0))
            def _():
                z_copy(zb, b, 0).wait_send()

            for stage in (P1, H1, P2, H2):
                for side in range(2):
                    copies(stage, side).wait_send()
            plane().wait_send()
        return carry

    lax.fori_loop(0, 8, drain, 0)
    for q in range(RADIUS):
        strip(0, q).wait_send()
        strip(1, q).wait_send()
    for part in range(3):
        for side in range(2):
            column(part, side).wait_send()


def body(latent, filters, widths, mix_weight, mix_bias):
    shifts = jnp.arange(2 * REACH + 1, dtype=jnp.int32) - REACH
    inside = jnp.abs(shifts)[None, None, :] <= widths[:, :, None]
    coefficients = jnp.where(inside[None], filters, jnp.zeros((), filters.dtype))
    coefficients = jnp.transpose(coefficients, (1, 0, 2, 3))
    weight = mix_weight[:, :, 0]
    packed = jnp.concatenate(
        [
            weight[:, :MAIN].reshape(45, 128),
            jnp.pad(weight[:, MAIN], (0, 128 - BASES))[None],
            jnp.zeros((2, 128), BF),
        ]
    )
    vmem = pl.BlockSpec(memory_space=pltpu.VMEM)
    dma = pltpu.SemaphoreType.DMA
    out = pl.pallas_call(
        body_kernel,
        out_shape=jax.ShapeDtypeStruct((256, 512), BF),
        in_specs=[vmem] * 4,
        out_specs=vmem,
        scratch_shapes=[
            pltpu.VMEM((4, 2, 2, 4, 8, 48, 128), BF),
            pltpu.VMEM((24, SPAN, MAIN + 1), BF),
            pltpu.VMEM((8, 288, 512), BF),
            pltpu.VMEM((256, 46 * 128), BF),
            pltpu.VMEM((512, 46 * 128), BF),
            dma((6, 16, 2)),
            dma((6, 16, 2)),
            dma((3, 2)),
            dma((3, 2)),
            dma((2, RADIUS)),
            dma((2,)),
            dma((2,)),
        ],
        compiler_params=pltpu.CompilerParams(
            collective_id=0, has_side_effects=True, vmem_limit_bytes=60 << 20
        ),
        name="sphere",
    )(packed, latent, coefficients, mix_bias[None])
    return out.reshape(16, 16, 512)


def solution(mesh):
    placed = (
        P("lat", "lon", None),
        P(None, "lat", None, None),
        P("lat", None),
        P(None, None, ("lat", "lon")),
        P(),
    )
    return jax.shard_map(
        body, mesh=mesh, in_specs=placed, out_specs=P("lat", "lon", None), check_vma=False
    )
```

```python
import math

import jax
import jax.numpy as jnp
from jax import lax
from jax.experimental import pallas as pl
from jax.experimental.pallas import tpu as pltpu
from jax.sharding import PartitionSpec as P

RADIUS = 4
REACH = 16
BASES = 9
MAIN = 640
SPAN = 48
DEPTH = 46 * 128
MESH = pl.DeviceIdType.MESH
BF = jnp.bfloat16
F32 = jnp.float32

Z1, P1, P2, H2, DD = range(5)
OWN, OUTER, INNER = range(3)


def device_of(x, y, z, core):
    return (x * 4 + (z // 8) * 2 + core, y * 8 + z % 8)


def prepare_kernel(w_ref, tail_ref, packed_ref, extra_ref, rows_ref):
    w = w_ref[0].astype(F32)
    for t in range(5):
        rows_ref[t * BASES : (t + 1) * BASES, :] = w[:, t * 128 : (t + 1) * 128]
    lane = lax.broadcasted_iota(jnp.int32, (BASES, 128), 1)
    row = lax.broadcasted_iota(jnp.int32, (BASES, 128), 0)
    last = jnp.where(lane == row, jnp.broadcast_to(w[:, MAIN:], (BASES, 128)), 0.0)
    rows_ref[45:46, :] = jnp.sum(last, axis=0, keepdims=True)
    rows_ref[46:48, :] = jnp.zeros((2, 128), F32)
    packed_ref[...] = rows_ref[...].astype(BF)
    lane = lax.broadcasted_iota(jnp.int32, (16, 128), 1)
    extra = jnp.zeros((16, 128), F32)
    for r in range(16):
        column = tail_ref[r, :, 0:1].astype(F32)
        extra = jnp.where(lane == RADIUS + r, jnp.broadcast_to(column, (16, 128)), extra)
    extra_ref[...] = extra.astype(BF)


def mask_taps(filters_ref, widths_ref, taps_ref):
    lane = lax.broadcasted_iota(jnp.int32, (16, 128), 1)
    inside = [
        jnp.abs(lane - REACH) <= jnp.broadcast_to(widths_ref[:, d : d + 1], (16, 128))
        for d in range(2 * RADIUS + 1)
    ]
    for k in range(BASES):
        taps = filters_ref[k].astype(F32)
        taps = jnp.pad(taps, ((0, 0), (0, 0), (0, 128 - taps.shape[2])))
        taps = jnp.stack([jnp.where(inside[d], taps[d], 0.0) for d in range(2 * RADIUS + 1)])
        taps_ref[k] = jnp.transpose(taps, (1, 0, 2))


def build_rows(taps_ref, a_ref, pair):
    lane = lax.broadcasted_iota(jnp.int32, (16, 128), 1)
    zero = jnp.zeros((16, 128), F32)
    for s in range(2):
        i = pair * 2 + s
        for k in range(BASES):
            taps = taps_ref[k, i]
            tiles = [None] * 4

            def put(t, part):
                tiles[t] = part if tiles[t] is None else tiles[t] + part

            for d in range(2 * RADIUS + 1):
                first, at = divmod(SPAN * (d + s), 128)
                line = jnp.broadcast_to(taps[d : d + 1], (16, 128))
                line = pltpu.roll(line, at, 1, stride=1, stride_axis=0)
                if at + SPAN > 128:
                    put(first, jnp.where(lane >= at, line, zero))
                    put(first + 1, jnp.where(lane < at, line, zero))
                else:
                    put(first, line)
            rows = pl.ds((s * BASES + k) * 16, 16)
            a_ref[pair, rows, :] = jnp.concatenate(tiles, 1).astype(BF)


def stencil_rows(a_ref, e_ref, f_ref, pair):
    lane = lax.broadcasted_iota(jnp.int32, (16, 128), 1)
    slab = e_ref[pl.ds(pair * 2, 10)].reshape(10 * SPAN, MAIN + 128)
    found = jnp.dot(a_ref[pair][:, : 10 * SPAN], slab, preferred_element_type=F32)
    for s in range(2):
        rows = pl.ds(pl.multiple_of((pair * 2 + s) * 16, 16), 16)
        last = jnp.zeros((16, 128), F32)
        for k in range(BASES):
            part = found[(s * BASES + k) * 16 : (s * BASES + k + 1) * 16]
            for t in range(5):
                h = t * BASES + k
                f_ref[rows, h * 128 : (h + 1) * 128] = part[:, t * 128 : (t + 1) * 128].astype(BF)
            tail = jnp.sum(part[:, MAIN:], axis=1, keepdims=True)
            last = jnp.where(lane == k, jnp.broadcast_to(tail, (16, 128)), last)
        f_ref[rows, 45 * 128 :] = last.astype(BF)


def main_kernel(
    w_in, extra, latent, filters_ref, widths_ref, bias_ref, out_ref,
    g_ref, e_ref, x_ref, taps_ref, a_ref, f_ref, wt_ref,
    send, recv, csend, crecv, xsend, xrecv, osend, orecv, own_sem,
):
    lat, lon = lax.axis_index("lat"), lax.axis_index("lon")
    x, core = lat // 4, lat % 2
    y = lon // 8
    z = ((lat // 2) % 2) * 8 + lon % 8
    xs = ((x + 3) % 4, (x + 1) % 4, (x + 2) % 4)
    ys = ((y + 3) % 4, (y + 1) % 4, (y + 2) % 4)
    to_x = [device_of(v, y, z, core) for v in xs]
    to_y = [device_of(x, v, z, core) for v in ys]
    to_z = [device_of(x, y, v, core) for v in ((z + 15) % 16, (z + 1) % 16)]
    sibling = (lat + 1 - 2 * core, lon)
    to_lon = [(lat, (lon + 31) % 32), (lat, (lon + 1) % 32)]
    top, bottom = lat == 0, lat == 15
    pole = top | bottom
    beyond = (
        jnp.where(pole, lat, lat - 1 + 2 * core),
        jnp.where(pole, (lon + 16) % 32, lon),
    )

    barrier = pltpu.get_barrier_semaphore()
    peers = to_x + to_y + to_z + [sibling] + to_lon + [beyond]
    for peer in peers:
        pl.semaphore_signal(barrier, inc=1, device_id=peer, device_id_type=MESH)
    pl.semaphore_wait(barrier, len(peers))

    def remote(src, dst, s, r, where):
        return pltpu.make_async_remote_copy(
            src_ref=src, dst_ref=dst, send_sem=s, recv_sem=r,
            device_id=where, device_id_type=MESH,
        )

    main = pl.ds(0, MAIN)
    centre = pl.ds(16, 16)

    def column(n, side):
        rows = pl.ds(RADIUS + 2 * n, 2)
        dst = e_ref.at[rows, pl.ds(32 * (1 - side), 16), main]
        return remote(
            latent.at[pl.ds(2 * n, 2), :, main], dst,
            csend.at[n, side], crecv.at[n, side], to_lon[side],
        )

    def outer_column(m, side):
        rows = pl.ds(20 * core + 2 * m, 2)
        dst = e_ref.at[rows, pl.ds(32 * (1 - side), 16), main]
        return remote(
            e_ref.at[rows, centre, main], dst,
            csend.at[8 + m, side], crecv.at[8 + m, side], to_lon[side],
        )

    def strip(q):
        row = jnp.where(pole, jnp.where(core == 0, 3 - q, 23 - q), jnp.where(core == 0, 20 + q, q))
        return remote(
            latent.at[12 * core + q, :, main], e_ref.at[row, centre, main],
            osend.at[q], orecv.at[0], beyond,
        )

    def extra_beyond():
        return remote(extra, x_ref.at[OUTER, centre, :], xsend.at[2], xrecv.at[2], beyond)

    def extra_column(part, side):
        src = extra if part == OWN else x_ref.at[OUTER, centre, :]
        dst = x_ref.at[part, pl.ds(32 * (1 - side), 16), :]
        return remote(src, dst, xsend.at[3 * part + side], xrecv.at[3 * part + side], to_lon[side])

    def inner_rows():
        src = e_ref.at[pl.ds(16 - 12 * core, RADIUS), :, main]
        dst = e_ref.at[pl.ds(20 * core, RADIUS), :, main]
        return remote(src, dst, xsend.at[5], xrecv.at[5], sibling)

    def inner_extra():
        return remote(x_ref.at[OWN], x_ref.at[INNER], xsend.at[6], xrecv.at[6], sibling)

    def block(zb):
        return g_ref.at[x, zb // 8, core, y, zb % 8]

    def z_copy(zb, b, side, src=None):
        return remote(
            block(zb) if src is None else src, block(zb),
            send.at[Z1, b, 0], recv.at[Z1, b, 0], to_z[side],
        )

    z_copy(z, 2, 0, w_in).start()
    z_copy(z, 1, 1, w_in).start()
    extra_beyond().start()
    for q in range(RADIUS):
        strip(q).start()
    for side in range(2):
        extra_column(OWN, side).start()
    own = [
        pltpu.make_async_copy(w_in, block(z), own_sem.at[0]),
        pltpu.make_async_copy(
            latent.at[:, :, main], e_ref.at[pl.ds(RADIUS, 16), centre, main], own_sem.at[1]
        ),
        pltpu.make_async_copy(extra, x_ref.at[OWN, centre, :], own_sem.at[2]),
    ]
    for copy in own:
        copy.start()
    own[0].wait()
    mask_taps(filters_ref, widths_ref, taps_ref)

    def pieces(i, odd):
        b = 2 * i + odd
        zb = (z + 15 - i) % 16 if odd else (z + i) % 16
        hi, lo = zb // 8, zb % 8
        near, far = (ys, xs) if odd else (xs, ys)
        to_near, to_far = (to_y, to_x) if odd else (to_x, to_y)
        me = (y, x) if odd else (x, y)
        pairs = (pl.ds(0, 2), pl.ds(2, 2))

        def one(v):
            return g_ref.at[x, hi, core, v, lo] if odd else g_ref.at[v, hi, core, y, lo]

        def line(v, part=slice(None)):
            return g_ref.at[v, hi, core, part, lo] if odd else g_ref.at[part, hi, core, v, lo]

        def sem(stage, slot):
            return send.at[stage, b, slot], recv.at[stage, b, slot]

        def copies(stage, side, incoming=False):
            slot = (1, 0, 2)[side] if incoming else side
            if stage == P1:
                v = near[side] if incoming else me[0]
                return remote(one(v), one(v), *sem(P1, slot), to_near[side])
            if stage == P2:
                v = far[side] if incoming else me[1]
                return remote(line(v), line(v), *sem(P2, slot), to_far[side])
            v = far[2] if incoming else far[1 - side]
            part = pairs[0] if slot == 1 else pairs[1]
            return remote(line(v, part), line(v, part), *sem(H2, slot), to_far[side])

        def plane():
            src = g_ref.at[:, hi, core, :, lo]
            return remote(src, src, send.at[DD, b, 0], recv.at[DD, b, 0], sibling)

        return b, zb, copies, plane

    def from_sibling(i, odd):
        b = 2 * i + odd
        zb = (z + 15 - i) % 16 if odd else (z + i) % 16
        dst = g_ref.at[:, zb // 8, 1 - core, :, zb % 8]
        return remote(dst, dst, send.at[DD, b, 0], recv.at[DD, b, 0], sibling)

    def step(t, carry):
        @pl.when(t < 8)
        def _():
            for odd in range(2):
                b, zb, copies, _ = pieces(t, odd)

                def arrive():
                    z_copy(zb, b, 0).wait_recv()

                if odd:
                    arrive()
                else:
                    pl.when(t > 0)(arrive)

                @pl.when(t < 7 if odd else (t < 7) & (t > 0))
                def _():
                    z_copy(zb, b + 2, odd).start()

                for side in range(3):
                    copies(P1, side).start()

        @pl.when(t < 5)
        def _():
            for side in range(2):
                column(t, side).start()

        @pl.when(t == 5)
        def _():
            rows = e_ref.at[pl.ds(20 * core, RADIUS), centre, main]
            pltpu.make_async_copy(rows, rows, orecv.at[0]).wait()
            extra_beyond().wait_recv()
            for side in range(2):
                extra_column(OUTER, side).start()

        @pl.when((t == 5) | (t == 6))
        def _():
            for side in range(2):
                outer_column(t - 5, side).start()

        @pl.when((t >= 7) & (t < 10))
        def _():
            for side in range(2):
                column(t - 2, side).start()

        @pl.when((t >= 1) & (t < 9))
        def _():
            for odd in range(2):
                _, _, copies, _ = pieces(t - 1, odd)
                for side in range(3):
                    copies(P1, side, True).wait_recv()
                for side in range(2):
                    copies(P2, side).start()

        @pl.when((t >= 3) & (t < 11))
        def _():
            for odd in range(2):
                _, _, copies, _ = pieces(t - 3, odd)
                for side in range(2):
                    copies(P2, 1 - side, True).wait_recv()
                    copies(H2, side).start()

        @pl.when(t >= 5)
        def _():
            for odd in range(2):
                _, _, copies, plane = pieces(t - 5, odd)
                for side in range(2):
                    copies(H2, side, True).wait_recv()
                plane().start()

        @pl.when(t < 8)
        def _():
            build_rows(taps_ref, a_ref, t)

        return carry

    lax.fori_loop(0, 13, step, 0)

    for copy in own[1:]:
        copy.wait()

    def columns_in(n, carry):
        for side in range(2):
            column(n, side).wait_recv()
        return carry

    lax.fori_loop(0, 8, columns_in, 0)
    for side in range(2):
        extra_column(OWN, side).wait_recv()
    inner_rows().start()
    inner_extra().start()

    lanes = lax.broadcasted_iota(jnp.int32, (SPAN, 128), 1)

    def spread(row, part, at):
        e_ref[row, :, MAIN:] = jnp.where(lanes == at, x_ref[part].astype(F32), 0.0).astype(BF)

    def spread_own(r, carry):
        spread(r, OWN, r)
        return carry

    def features(pair, carry):
        stencil_rows(a_ref, e_ref, f_ref, pair)
        return carry

    lax.fori_loop(RADIUS, RADIUS + 16, spread_own, 0)
    lax.fori_loop(2, 6, features, 0)

    for side in range(2):
        for m in range(2):
            outer_column(m, side).wait_recv()
        extra_column(OUTER, side).wait_recv()
    inner_back = e_ref.at[pl.ds(20 - 20 * core, RADIUS), :, main]
    remote(inner_back, inner_back, xsend.at[5], xrecv.at[5], sibling).wait_recv()
    inner_extra().wait_recv()
    for q in range(RADIUS):
        spread(q, 1 + core, jnp.where(top, 7 - q, 16 + q))
        spread(20 + q, 2 - core, jnp.where(bottom, 19 - q, 4 + q))
    lax.fori_loop(0, 2, features, 0)
    lax.fori_loop(6, 8, features, 0)

    def wait_planes(i, carry):
        for odd in range(2):
            from_sibling(i, odd).wait_recv()
        return carry

    lax.fori_loop(0, 8, wait_planes, 0)

    def lay(n, carry):
        band, half = n // 2, n % 2
        rows = g_ref[band // 4, (band // 2) % 2, band % 2, pl.ds(half * 2, 2)]
        flat = rows.reshape(16, 48 * 128)
        wt_ref[pl.ds(pl.multiple_of(n * 16, 16), 16), :] = flat[:, :DEPTH]
        return carry

    lax.fori_loop(0, 32, lay, 0)

    def mix(n, carry):
        cols = pl.ds(pl.multiple_of(n * 256, 256), 256)
        total = lax.dot_general(
            f_ref[...], wt_ref[cols, :], (((1,), (1,)), ((), ())), preferred_element_type=F32
        )
        total = total + bias_ref[:, cols]
        value = 0.5 * total * (1.0 + lax.erf(total * math.sqrt(0.5)))
        out_ref[:, cols] = value.astype(BF)
        return carry

    lax.fori_loop(0, 2, mix, 0)

    def drain(i, carry):
        for odd in range(2):
            b, zb, copies, plane = pieces(i, odd)

            @pl.when((i >= 0) if odd else (i > 0))
            def _():
                z_copy(zb, b, 0).wait_send()

            for side in range(3):
                copies(P1, side).wait_send()
            for side in range(2):
                copies(P2, side).wait_send()
                copies(H2, side).wait_send()
            plane().wait_send()
        for side in range(2):
            column(i, side).wait_send()
        return carry

    lax.fori_loop(0, 8, drain, 0)
    for q in range(RADIUS):
        strip(q).wait_send()
    extra_beyond().wait_send()
    for side in range(2):
        for m in range(2):
            outer_column(m, side).wait_send()
        for part in (OWN, OUTER):
            extra_column(part, side).wait_send()
    inner_rows().wait_send()
    inner_extra().wait_send()


def body(latent, filters, widths, mix_weight, mix_bias):
    vmem = pl.BlockSpec(memory_space=pltpu.VMEM)
    packed, extra = pl.pallas_call(
        prepare_kernel,
        grid=(1,),
        out_shape=(jax.ShapeDtypeStruct((48, 128), BF), jax.ShapeDtypeStruct((16, 128), BF)),
        in_specs=[
            pl.BlockSpec((1, BASES, MAIN + 1), lambda i: (0, 0, 0)),
            pl.BlockSpec((16, 16, 128), lambda i: (0, 0, 5)),
        ],
        out_specs=(pl.BlockSpec((48, 128), lambda i: (0, 0)), pl.BlockSpec((16, 128), lambda i: (0, 0))),
        scratch_shapes=[pltpu.VMEM((48, 128), F32)],
        name="prepare",
    )(jnp.transpose(mix_weight, (2, 0, 1)), latent)
    dma = pltpu.SemaphoreType.DMA
    out = pl.pallas_call(
        main_kernel,
        out_shape=jax.ShapeDtypeStruct((256, 512), BF),
        in_specs=[vmem] * 6,
        out_specs=vmem,
        scratch_shapes=[
            pltpu.VMEM((4, 2, 2, 4, 8, 48, 128), BF),
            pltpu.VMEM((24, SPAN, MAIN + 128), BF),
            pltpu.VMEM((3, SPAN, 128), BF),
            pltpu.VMEM((BASES, 16, 2 * RADIUS + 1, 128), F32),
            pltpu.VMEM((8, 288, 512), BF),
            pltpu.VMEM((256, DEPTH), BF),
            pltpu.VMEM((512, DEPTH), BF),
            dma((5, 16, 3)),
            dma((5, 16, 3)),
            dma((10, 2)),
            dma((10, 2)),
            dma((7,)),
            dma((7,)),
            dma((RADIUS,)),
            dma((1,)),
            dma((3,)),
        ],
        compiler_params=pltpu.CompilerParams(
            collective_id=0, has_side_effects=True, vmem_limit_bytes=60 << 20
        ),
        name="sphere",
    )(packed, extra, latent, jnp.transpose(filters, (0, 2, 1, 3)), widths, mix_bias[None])
    return out.reshape(16, 16, 512)


def solution(mesh):
    placed = (
        P("lat", "lon", None),
        P(None, "lat", None, None),
        P("lat", None),
        P(None, None, ("lat", "lon")),
        P(),
    )
    return jax.shard_map(
        body, mesh=mesh, in_specs=placed, out_specs=P("lat", "lon", None), check_vma=False
    )
```

```python
import math

import jax
import jax.numpy as jnp
from jax import lax
from jax.experimental import pallas as pl
from jax.experimental.pallas import tpu as pltpu
from jax.sharding import PartitionSpec as P

RADIUS = 4
REACH = 16
BASES = 9
MAIN = 640
SPAN = 48
DEPTH = 46 * 128
MESH = pl.DeviceIdType.MESH
BF = jnp.bfloat16
F32 = jnp.float32

Z1, P1, P2, DD = range(4)
OWN, OUTER, INNER = range(3)
STRIPS_AT = 6
INNER_AT = 5


def device_of(x, y, z, core):
    return (x * 4 + (z // 8) * 2 + core, y * 8 + z % 8)


def prepare(w_ref, latent, packed_ref, extra_ref, rows_ref):
    w = w_ref[0].astype(F32)
    for t in range(5):
        rows_ref[t * BASES : (t + 1) * BASES, :] = w[:, t * 128 : (t + 1) * 128]
    lane = lax.broadcasted_iota(jnp.int32, (BASES, 128), 1)
    row = lax.broadcasted_iota(jnp.int32, (BASES, 128), 0)
    last = jnp.where(lane == row, jnp.broadcast_to(w[:, MAIN:], (BASES, 128)), 0.0)
    rows_ref[45:46, :] = jnp.sum(last, axis=0, keepdims=True)
    rows_ref[46:48, :] = jnp.zeros((2, 128), F32)
    packed_ref[...] = rows_ref[...].astype(BF)
    lane = lax.broadcasted_iota(jnp.int32, (16, 128), 1)
    extra = jnp.zeros((16, 128), F32)
    for r in range(16):
        column = latent[r, :, MAIN:].astype(F32)
        extra = jnp.where(lane == RADIUS + r, jnp.broadcast_to(column, (16, 128)), extra)
    extra_ref[...] = extra.astype(BF)


def mask_taps(filters_ref, widths_ref, taps_ref):
    lane = lax.broadcasted_iota(jnp.int32, (16, 128), 1)
    inside = [
        jnp.abs(lane - REACH) <= jnp.broadcast_to(widths_ref[:, d : d + 1], (16, 128))
        for d in range(2 * RADIUS + 1)
    ]
    for k in range(BASES):
        taps = filters_ref[k].astype(F32)
        taps = jnp.pad(taps, ((0, 0), (0, 0), (0, 128 - taps.shape[2])))
        taps = jnp.stack([jnp.where(inside[d], taps[d], 0.0) for d in range(2 * RADIUS + 1)])
        taps_ref[k] = jnp.transpose(taps, (1, 0, 2))


def build_rows(taps_ref, a_ref, pair):
    lane = lax.broadcasted_iota(jnp.int32, (16, 128), 1)
    zero = jnp.zeros((16, 128), F32)
    for s in range(2):
        i = pair * 2 + s
        for k in range(BASES):
            taps = taps_ref[k, i]
            tiles = [None] * 4

            def put(t, part):
                tiles[t] = part if tiles[t] is None else tiles[t] + part

            for d in range(2 * RADIUS + 1):
                first, at = divmod(SPAN * (d + s), 128)
                line = jnp.broadcast_to(taps[d : d + 1], (16, 128))
                line = pltpu.roll(line, at, 1, stride=1, stride_axis=0)
                if at + SPAN > 128:
                    put(first, jnp.where(lane >= at, line, zero))
                    put(first + 1, jnp.where(lane < at, line, zero))
                else:
                    put(first, line)
            rows = pl.ds((s * BASES + k) * 16, 16)
            a_ref[pair, rows, :] = jnp.concatenate(tiles, 1).astype(BF)


def stencil_rows(a_ref, e_ref, f_ref, pair):
    lane = lax.broadcasted_iota(jnp.int32, (16, 128), 1)
    slab = e_ref[pl.ds(pair * 2, 10)].reshape(10 * SPAN, MAIN + 128)
    found = jnp.dot(a_ref[pair][:, : 10 * SPAN], slab, preferred_element_type=F32)
    for s in range(2):
        rows = pl.ds(pl.multiple_of((pair * 2 + s) * 16, 16), 16)
        last = jnp.zeros((16, 128), F32)
        for k in range(BASES):
            part = found[(s * BASES + k) * 16 : (s * BASES + k + 1) * 16]
            for t in range(5):
                h = t * BASES + k
                f_ref[rows, h * 128 : (h + 1) * 128] = part[:, t * 128 : (t + 1) * 128].astype(BF)
            tail = jnp.sum(part[:, MAIN:], axis=1, keepdims=True)
            last = jnp.where(lane == k, jnp.broadcast_to(tail, (16, 128)), last)
        f_ref[rows, 45 * 128 :] = last.astype(BF)


def main_kernel(
    w_ref, latent, filters_ref, widths_ref, bias_ref, out_ref,
    w_in, extra, rows_ref, g_ref, e_ref, x_ref, taps_ref, a_ref, f_ref, wt_ref, perm_ref, value_ref,
    send, recv, csend, crecv, xsend, xrecv, osend, orecv, own_sem,
):
    lat, lon = lax.axis_index("lat"), lax.axis_index("lon")
    x, core = lat // 4, lat % 2
    y = lon // 8
    z = ((lat // 2) % 2) * 8 + lon % 8
    xs = ((x + 3) % 4, (x + 1) % 4, (x + 2) % 4)
    ys = ((y + 3) % 4, (y + 1) % 4, (y + 2) % 4)
    to_x = [device_of(v, y, z, core) for v in xs]
    to_y = [device_of(x, v, z, core) for v in ys]
    to_z = [[device_of(x, y, (z + 16 + d * n) % 16, core) for d in (-1, 1)] for n in range(1, 9)]
    sibling = (lat + 1 - 2 * core, lon)
    to_lon = [(lat, (lon + 31) % 32), (lat, (lon + 1) % 32)]
    top, bottom = lat == 0, lat == 15
    pole = top | bottom
    beyond = (
        jnp.where(pole, lat, lat - 1 + 2 * core),
        jnp.where(pole, (lon + 16) % 32, lon),
    )

    barrier = pltpu.get_barrier_semaphore()
    peers = to_x + to_y + sum(to_z[:7], []) + to_z[7][:1] + [sibling] + to_lon + [beyond]
    for peer in peers:
        pl.semaphore_signal(barrier, inc=1, device_id=peer, device_id_type=MESH)
    prepare(w_ref, latent, w_in, extra, rows_ref)
    mask_taps(filters_ref, widths_ref, taps_ref)
    pl.semaphore_wait(barrier, len(peers))

    def remote(src, dst, s, r, where):
        return pltpu.make_async_remote_copy(
            src_ref=src, dst_ref=dst, send_sem=s, recv_sem=r,
            device_id=where, device_id_type=MESH,
        )

    main = pl.ds(0, MAIN)
    centre = pl.ds(16, 16)

    def column(c, side):
        n = jnp.where(core == 0, 7 - c, c)
        rows = pl.ds(RADIUS + 2 * n, 2)
        dst = e_ref.at[rows, pl.ds(32 * (1 - side), 16), main]
        return remote(
            latent.at[pl.ds(2 * n, 2), :, main], dst,
            csend.at[c, side], crecv.at[c, side], to_lon[side],
        )

    def outer_column(m, side):
        rows = pl.ds(20 * core + 2 * m, 2)
        dst = e_ref.at[rows, pl.ds(32 * (1 - side), 16), main]
        return remote(
            e_ref.at[rows, centre, main], dst,
            csend.at[8 + m, side], crecv.at[8 + m, side], to_lon[side],
        )

    def strip(q):
        row = jnp.where(pole, jnp.where(core == 0, 3 - q, 23 - q), jnp.where(core == 0, 20 + q, q))
        return remote(
            latent.at[12 * core + q, :, main], e_ref.at[row, centre, main],
            osend.at[q], orecv.at[0], beyond,
        )

    def extra_beyond():
        return remote(extra, x_ref.at[OUTER, centre, :], xsend.at[2], xrecv.at[2], beyond)

    def extra_column(part, side):
        src = extra if part == OWN else x_ref.at[OUTER, centre, :]
        dst = x_ref.at[part, pl.ds(32 * (1 - side), 16), :]
        return remote(src, dst, xsend.at[3 * part + side], xrecv.at[3 * part + side], to_lon[side])

    def inner_rows():
        src = e_ref.at[pl.ds(16 - 12 * core, RADIUS), :, main]
        dst = e_ref.at[pl.ds(20 * core, RADIUS), :, main]
        return remote(src, dst, xsend.at[5], xrecv.at[5], sibling)

    def inner_extra():
        return remote(x_ref.at[OWN], x_ref.at[INNER], xsend.at[6], xrecv.at[6], sibling)

    def block(b):
        return g_ref.at[b, core, x, y]

    def z_copy(b, side, hops=1):
        return remote(w_in, block(b), send.at[Z1, b, 0], recv.at[Z1, b, 0], to_z[hops - 1][side])

    for hops in range(1, 9):
        for side in range(2):
            if hops < 8 or side == 1:
                z_copy(2 * hops - side, side, hops).start()
    own = [
        pltpu.make_async_copy(w_in, block(0), own_sem.at[0]),
        pltpu.make_async_copy(
            latent.at[:, :, main], e_ref.at[pl.ds(RADIUS, 16), centre, main], own_sem.at[1]
        ),
        pltpu.make_async_copy(extra, x_ref.at[OWN, centre, :], own_sem.at[2]),
    ]
    for copy in own:
        copy.start()
    own[0].wait()

    def pieces(i, odd):
        b = 2 * i + odd
        near, far = (ys, xs) if odd else (xs, ys)
        to_near, to_far = (to_y, to_x) if odd else (to_x, to_y)
        me = (y, x) if odd else (x, y)

        def one(v):
            return g_ref.at[b, core, x, v] if odd else g_ref.at[b, core, v, y]

        def line(v):
            return g_ref.at[b, core, v] if odd else g_ref.at[b, core, :, v]

        def sem(stage, slot):
            return send.at[stage, b, slot], recv.at[stage, b, slot]

        def copies(stage, side, incoming=False):
            slot = (1, 0, 2)[side] if incoming else side
            if stage == P1:
                v = near[side] if incoming else me[0]
                return remote(one(v), one(v), *sem(P1, slot), to_near[side])
            v = far[side] if incoming else me[1]
            return remote(line(v), line(v), *sem(P2, slot), to_far[side])

        def plane():
            src = g_ref.at[b, core]
            return remote(src, src, send.at[DD, b, 0], recv.at[DD, b, 0], sibling)

        return b, copies, plane

    def from_sibling(b):
        dst = g_ref.at[b, 1 - core]
        return remote(dst, dst, send.at[DD, b, 0], recv.at[DD, b, 0], sibling)

    def lay(b, c):
        flat = g_ref[b, c].reshape(16, 48 * 128)
        wt_ref[pl.ds(pl.multiple_of((b * 2 + c) * 16, 16), 16), :] = flat[:, :DEPTH]

    def planar(i, odd):
        _, copies, _ = pieces(i, odd)
        for side in range(3):
            copies(P1, side).start()

    planar(0, 0)
    for q in range(RADIUS):
        strip(q).start()
    extra_beyond().start()
    for side in range(2):
        extra_column(OWN, side).start()

    def every(c, carry):
        for side in range(2):
            column(c, side).start()
        return carry

    lax.fori_loop(0, 8, every, 0)

    def arrive(t, odd):
        z_copy(2 * t + odd, 0).wait_recv()
        planar(t, odd)

    def first(t, carry):
        pl.when(t > 0)(lambda: arrive(t, 0))
        arrive(t, 1)
        return carry

    def step(u, carry):
        @pl.when(u < 8)
        def _():
            for odd in range(2):
                _, copies, _ = pieces(u, odd)
                for side in range(3):
                    copies(P1, side, True).wait_recv()
                for side in range(3):
                    copies(P2, side).start()

        @pl.when(u < 4)
        def _():
            for odd in range(2):
                arrive(u + 4, odd)

        @pl.when(u == STRIPS_AT)
        def _():
            rows = e_ref.at[pl.ds(20 * core, RADIUS), centre, main]
            pltpu.make_async_copy(rows, rows, orecv.at[0]).wait()
            extra_beyond().wait_recv()
            for side in range(2):
                extra_column(OUTER, side).start()
                for m in range(2):
                    outer_column(m, side).start()

        @pl.when((u >= 2) & (u < 10))
        def _():
            for odd in range(2):
                b, copies, plane = pieces(u - 2, odd)
                for side in range(3):
                    copies(P2, side, True).wait_recv()
                plane().start()
                lay(b, core)

        @pl.when((u >= 3) & (u < 10))
        def _():
            for odd in range(2):
                b = 2 * (u - 3) + odd
                from_sibling(b).wait_recv()
                lay(b, 1 - core)

        @pl.when(u < 8)
        def _():
            build_rows(taps_ref, a_ref, u)

        @pl.when(u == INNER_AT)
        def _():
            own[1].wait()
            own[2].wait()
            for side in range(2):
                for c in range(2):
                    column(c, side).wait_recv()
                extra_column(OWN, side).wait_recv()
            inner_rows().start()
            inner_extra().start()

        @pl.when(u == 7)
        def _():
            inner_back = e_ref.at[pl.ds(20 - 20 * core, RADIUS), :, main]
            remote(inner_back, inner_back, xsend.at[5], xrecv.at[5], sibling).wait_recv()
            inner_extra().wait_recv()
            for q in range(RADIUS):
                top_lane = jnp.where(top, 7 - q, 16 + q)
                low_lane = jnp.where(bottom, 19 - q, 4 + q)
                spread(20 - 20 * core + q, INNER, jnp.where(core == 0, low_lane, top_lane))
            lax.fori_loop(RADIUS, RADIUS + 16, spread_own, 0)

        @pl.when((u >= 7) & (u < 10))
        def _():
            def early(k, c):
                n = 2 * (u - 7) + k
                for side in range(2):
                    column(n + 2, side).wait_recv()
                return features(n, c)

            lax.fori_loop(0, 2, early, 0)

        return carry

    lanes = lax.broadcasted_iota(jnp.int32, (SPAN, 128), 1)

    def spread(row, part, at):
        e_ref[row, :, MAIN:] = jnp.where(lanes == at, x_ref[part].astype(F32), 0.0).astype(BF)

    def spread_own(r, carry):
        spread(r, OWN, r)
        return carry

    def features(n, carry):
        stencil_rows(a_ref, e_ref, f_ref, jnp.where(core == 0, 7 - n, n))
        return carry

    def places(n, carry):
        i, odd, c = n // 4, (n // 2) % 2, n % 2
        place = jnp.where(odd == 1, z + 15 - i, z + i) % 16
        row = lax.broadcasted_iota(jnp.int32, (16, 512), 0)
        channel = lax.broadcasted_iota(jnp.int32, (16, 512), 1)
        at = (row >> 2) * 128 + (row & 3) * 8 + ((place // 8) * 64 + c * 32 + place % 8)
        perm_ref[pl.ds(pl.multiple_of(n * 16, 16), 16), :] = jnp.where(channel == at, 1.0, 0.0).astype(BF)
        return carry

    lax.fori_loop(0, 32, places, 0)

    lax.fori_loop(0, 4, first, 0)
    lax.fori_loop(0, 10, step, 0)

    for side in range(2):
        for m in range(2):
            outer_column(m, side).wait_recv()
        extra_column(OUTER, side).wait_recv()
    for q in range(RADIUS):
        top_lane = jnp.where(top, 7 - q, 16 + q)
        low_lane = jnp.where(bottom, 19 - q, 4 + q)
        spread(20 * core + q, OUTER, jnp.where(core == 0, top_lane, low_lane))
    lax.fori_loop(6, 8, features, 0)

    def mix(n, carry):
        @pl.when(n == 1)
        def _():
            for b in (14, 15):
                from_sibling(b).wait_recv()
                lay(b, 1 - core)

        cols = pl.ds(pl.multiple_of(n * 256, 256), 256)
        total = lax.dot_general(
            f_ref[...], wt_ref[cols, :], (((1,), (1,)), ((), ())), preferred_element_type=F32
        )
        bias = lax.dot_general(
            bias_ref[...], perm_ref[cols, :].astype(F32), (((1,), (1,)), ((), ())),
            precision=lax.Precision.HIGHEST, preferred_element_type=F32,
        )
        total = total + bias
        value = 0.5 * total * (1.0 + lax.erf(total * math.sqrt(0.5)))
        value_ref[:, cols] = value.astype(BF)
        return carry

    lax.fori_loop(0, 2, mix, 0)
    out_ref[...] = jnp.dot(
        value_ref[...], perm_ref[...], preferred_element_type=F32
    ).astype(BF)

    def drain(i, carry):
        for odd in range(2):
            b, copies, plane = pieces(i, odd)

            @pl.when((i >= 0) if odd else (i > 0))
            def _():
                z_copy(b, 0).wait_send()

            for side in range(3):
                copies(P1, side).wait_send()
                copies(P2, side).wait_send()
            plane().wait_send()
        for side in range(2):
            column(i, side).wait_send()
        return carry

    lax.fori_loop(0, 8, drain, 0)
    for q in range(RADIUS):
        strip(q).wait_send()
    extra_beyond().wait_send()
    for side in range(2):
        for m in range(2):
            outer_column(m, side).wait_send()
        for part in (OWN, OUTER):
            extra_column(part, side).wait_send()
    inner_rows().wait_send()
    inner_extra().wait_send()


def body(latent, filters, widths, mix_weight, mix_bias):
    vmem = pl.BlockSpec(memory_space=pltpu.VMEM)
    dma = pltpu.SemaphoreType.DMA
    out = pl.pallas_call(
        main_kernel,
        out_shape=jax.ShapeDtypeStruct((256, 512), BF),
        in_specs=[vmem] * 5,
        out_specs=vmem,
        scratch_shapes=[
            pltpu.VMEM((48, 128), BF),
            pltpu.VMEM((16, 128), BF),
            pltpu.VMEM((48, 128), F32),
            pltpu.VMEM((16, 2, 4, 4, 48, 128), BF),
            pltpu.VMEM((24, SPAN, MAIN + 128), BF),
            pltpu.VMEM((3, SPAN, 128), BF),
            pltpu.VMEM((BASES, 16, 2 * RADIUS + 1, 128), F32),
            pltpu.VMEM((8, 288, 512), BF),
            pltpu.VMEM((256, DEPTH), BF),
            pltpu.VMEM((512, DEPTH), BF),
            pltpu.VMEM((512, 512), BF),
            pltpu.VMEM((256, 512), BF),
            dma((4, 16, 3)),
            dma((4, 16, 3)),
            dma((10, 2)),
            dma((10, 2)),
            dma((7,)),
            dma((7,)),
            dma((RADIUS,)),
            dma((1,)),
            dma((3,)),
        ],
        compiler_params=pltpu.CompilerParams(
            collective_id=0, has_side_effects=True, vmem_limit_bytes=60 << 20
        ),
        name="sphere",
    )(
        jnp.transpose(mix_weight, (2, 0, 1)),
        latent,
        jnp.transpose(filters, (0, 2, 1, 3)),
        widths,
        mix_bias[None],
    )
    return out.reshape(16, 16, 512)


def solution(mesh):
    placed = (
        P("lat", "lon", None),
        P(None, "lat", None, None),
        P("lat", None),
        P(None, None, ("lat", "lon")),
        P(),
    )
    return jax.shard_map(
        body, mesh=mesh, in_specs=placed, out_specs=P("lat", "lon", None), check_vma=False
    )
```

```python
import math

import jax
import jax.numpy as jnp
from jax import lax
from jax.experimental import pallas as pl
from jax.experimental.pallas import tpu as pltpu
from jax.sharding import PartitionSpec as P

RADIUS = 4
REACH = 16
BASES = 9
MAIN = 640
SPAN = 48
DEPTH = 46 * 128
MESH = pl.DeviceIdType.MESH
BF = jnp.bfloat16
F32 = jnp.float32

Z1, P1, P2, DD = range(4)
OWN, OUTER, INNER = range(3)
STRIPS_AT = 6
INNER_AT = 5


def device_of(x, y, z, core):
    return (x * 4 + (z // 8) * 2 + core, y * 8 + z % 8)


def prepare(w_ref, latent, packed_ref, extra_ref, rows_ref):
    w = w_ref[0].astype(F32)
    for t in range(5):
        rows_ref[t * BASES : (t + 1) * BASES, :] = w[:, t * 128 : (t + 1) * 128]
    lane = lax.broadcasted_iota(jnp.int32, (BASES, 128), 1)
    row = lax.broadcasted_iota(jnp.int32, (BASES, 128), 0)
    last = jnp.where(lane == row, jnp.broadcast_to(w[:, MAIN:], (BASES, 128)), 0.0)
    rows_ref[45:46, :] = jnp.sum(last, axis=0, keepdims=True)
    rows_ref[46:48, :] = jnp.zeros((2, 128), F32)
    packed_ref[...] = rows_ref[...].astype(BF)
    lane = lax.broadcasted_iota(jnp.int32, (16, 128), 1)
    extra = jnp.zeros((16, 128), F32)
    for r in range(16):
        column = latent[r, :, MAIN:].astype(F32)
        extra = jnp.where(lane == RADIUS + r, jnp.broadcast_to(column, (16, 128)), extra)
    extra_ref[...] = extra.astype(BF)


def mask_taps(filters_ref, widths_ref, taps_ref):
    lane = lax.broadcasted_iota(jnp.int32, (16, 128), 1)
    inside = [
        jnp.abs(lane - REACH) <= jnp.broadcast_to(widths_ref[:, d : d + 1], (16, 128))
        for d in range(2 * RADIUS + 1)
    ]
    for k in range(BASES):
        taps = filters_ref[k].astype(F32)
        taps = jnp.pad(taps, ((0, 0), (0, 0), (0, 128 - taps.shape[2])))
        taps = jnp.stack([jnp.where(inside[d], taps[d], 0.0) for d in range(2 * RADIUS + 1)])
        taps_ref[k] = jnp.transpose(taps, (1, 0, 2))


def build_rows(taps_ref, a_ref, pair):
    lane = lax.broadcasted_iota(jnp.int32, (16, 128), 1)
    zero = jnp.zeros((16, 128), F32)
    for s in range(2):
        i = pair * 2 + s
        for k in range(BASES):
            taps = taps_ref[k, i]
            tiles = [None] * 4

            def put(t, part):
                tiles[t] = part if tiles[t] is None else tiles[t] + part

            for d in range(2 * RADIUS + 1):
                first, at = divmod(SPAN * (d + s), 128)
                line = jnp.broadcast_to(taps[d : d + 1], (16, 128))
                line = pltpu.roll(line, at, 1, stride=1, stride_axis=0)
                if at + SPAN > 128:
                    put(first, jnp.where(lane >= at, line, zero))
                    put(first + 1, jnp.where(lane < at, line, zero))
                else:
                    put(first, line)
            rows = pl.ds((s * BASES + k) * 16, 16)
            a_ref[pair, rows, :] = jnp.concatenate(tiles, 1).astype(BF)


def stencil_rows(a_ref, e_ref, f_ref, pair):
    lane = lax.broadcasted_iota(jnp.int32, (16, 128), 1)
    slab = e_ref[pl.ds(pair * 2, 10)].reshape(10 * SPAN, MAIN + 128)
    found = jnp.dot(a_ref[pair][:, : 10 * SPAN], slab, preferred_element_type=F32)
    for s in range(2):
        rows = pl.ds(pl.multiple_of((pair * 2 + s) * 16, 16), 16)
        last = jnp.zeros((16, 128), F32)
        for k in range(BASES):
            part = found[(s * BASES + k) * 16 : (s * BASES + k + 1) * 16]
            for t in range(5):
                h = t * BASES + k
                f_ref[rows, h * 128 : (h + 1) * 128] = part[:, t * 128 : (t + 1) * 128].astype(BF)
            tail = jnp.sum(part[:, MAIN:], axis=1, keepdims=True)
            last = jnp.where(lane == k, jnp.broadcast_to(tail, (16, 128)), last)
        f_ref[rows, 45 * 128 :] = last.astype(BF)


def main_kernel(
    w_ref, latent, filters_ref, widths_ref, bias_ref, out_ref,
    w_in, extra, rows_ref, g_ref, e_ref, x_ref, taps_ref, a_ref, f_ref, wt_ref, perm_ref, value_ref,
    send, recv, csend, crecv, xsend, xrecv, osend, orecv, own_sem,
):
    lat, lon = lax.axis_index("lat"), lax.axis_index("lon")
    x, core = lat // 4, lat % 2
    y = lon // 8
    z = ((lat // 2) % 2) * 8 + lon % 8
    xs = ((x + 3) % 4, (x + 1) % 4, (x + 2) % 4)
    ys = ((y + 3) % 4, (y + 1) % 4, (y + 2) % 4)
    to_x = [device_of(v, y, z, core) for v in xs]
    to_y = [device_of(x, v, z, core) for v in ys]
    to_z = [[device_of(x, y, (z + 16 + d * n) % 16, core) for d in (-1, 1)] for n in range(1, 9)]
    sibling = (lat + 1 - 2 * core, lon)
    to_lon = [(lat, (lon + 31) % 32), (lat, (lon + 1) % 32)]
    top, bottom = lat == 0, lat == 15
    pole = top | bottom
    beyond = (
        jnp.where(pole, lat, lat - 1 + 2 * core),
        jnp.where(pole, (lon + 16) % 32, lon),
    )

    barrier = pltpu.get_barrier_semaphore()
    peers = to_x + to_y + sum(to_z[:7], []) + to_z[7][:1] + [sibling] + to_lon + [beyond]
    for peer in peers:
        pl.semaphore_signal(barrier, inc=1, device_id=peer, device_id_type=MESH)
    prepare(w_ref, latent, w_in, extra, rows_ref)
    mask_taps(filters_ref, widths_ref, taps_ref)
    pl.semaphore_wait(barrier, len(peers))

    def remote(src, dst, s, r, where):
        return pltpu.make_async_remote_copy(
            src_ref=src, dst_ref=dst, send_sem=s, recv_sem=r,
            device_id=where, device_id_type=MESH,
        )

    main = pl.ds(0, MAIN)
    centre = pl.ds(16, 16)

    def column(c, side):
        n = jnp.where(core == 0, 7 - c, c)
        rows = pl.ds(RADIUS + 2 * n, 2)
        dst = e_ref.at[rows, pl.ds(32 * (1 - side), 16), main]
        return remote(
            latent.at[pl.ds(2 * n, 2), :, main], dst,
            csend.at[c, side], crecv.at[c, side], to_lon[side],
        )

    def outer_column(m, side):
        rows = pl.ds(20 * core + 2 * m, 2)
        dst = e_ref.at[rows, pl.ds(32 * (1 - side), 16), main]
        return remote(
            e_ref.at[rows, centre, main], dst,
            csend.at[8 + m, side], crecv.at[8 + m, side], to_lon[side],
        )

    def strip(q):
        row = jnp.where(pole, jnp.where(core == 0, 3 - q, 23 - q), jnp.where(core == 0, 20 + q, q))
        return remote(
            latent.at[12 * core + q, :, main], e_ref.at[row, centre, main],
            osend.at[q], orecv.at[0], beyond,
        )

    def extra_beyond():
        return remote(extra, x_ref.at[OUTER, centre, :], xsend.at[2], xrecv.at[2], beyond)

    def extra_column(part, side):
        src = extra if part == OWN else x_ref.at[OUTER, centre, :]
        dst = x_ref.at[part, pl.ds(32 * (1 - side), 16), :]
        return remote(src, dst, xsend.at[3 * part + side], xrecv.at[3 * part + side], to_lon[side])

    def inner_rows():
        src = e_ref.at[pl.ds(16 - 12 * core, RADIUS), :, main]
        dst = e_ref.at[pl.ds(20 * core, RADIUS), :, main]
        return remote(src, dst, xsend.at[5], xrecv.at[5], sibling)

    def inner_extra():
        return remote(x_ref.at[OWN], x_ref.at[INNER], xsend.at[6], xrecv.at[6], sibling)

    def block(b):
        return g_ref.at[b, core, x, y]

    def z_copy(b, side, hops=1):
        return remote(w_in, block(b), send.at[Z1, b, 0], recv.at[Z1, b, 0], to_z[hops - 1][side])

    for hops in range(1, 9):
        for side in range(2):
            if hops < 8 or side == 1:
                z_copy(2 * hops - side, side, hops).start()
    own = [
        pltpu.make_async_copy(w_in, block(0), own_sem.at[0]),
        pltpu.make_async_copy(
            latent.at[:, :, main], e_ref.at[pl.ds(RADIUS, 16), centre, main], own_sem.at[1]
        ),
        pltpu.make_async_copy(extra, x_ref.at[OWN, centre, :], own_sem.at[2]),
    ]
    for copy in own:
        copy.start()
    own[0].wait()

    def pieces(i, odd):
        b = 2 * i + odd
        near, far = (ys, xs) if odd else (xs, ys)
        to_near, to_far = (to_y, to_x) if odd else (to_x, to_y)
        me = (y, x) if odd else (x, y)

        def one(v):
            return g_ref.at[b, core, x, v] if odd else g_ref.at[b, core, v, y]

        def line(v):
            return g_ref.at[b, core, v] if odd else g_ref.at[b, core, :, v]

        def sem(stage, slot):
            return send.at[stage, b, slot], recv.at[stage, b, slot]

        def copies(stage, side, incoming=False):
            slot = (1, 0, 2)[side] if incoming else side
            if stage == P1:
                v = near[side] if incoming else me[0]
                return remote(one(v), one(v), *sem(P1, slot), to_near[side])
            v = far[side] if incoming else me[1]
            return remote(line(v), line(v), *sem(P2, slot), to_far[side])

        def plane():
            src = g_ref.at[b, core]
            return remote(src, src, send.at[DD, b, 0], recv.at[DD, b, 0], sibling)

        return b, copies, plane

    def from_sibling(b):
        dst = g_ref.at[b, 1 - core]
        return remote(dst, dst, send.at[DD, b, 0], recv.at[DD, b, 0], sibling)

    def lay(b, c):
        flat = g_ref[b, c].reshape(16, 48 * 128)
        wt_ref[pl.ds(pl.multiple_of((b * 2 + c) * 16, 16), 16), :] = flat[:, :DEPTH]

    def planar(i, odd):
        _, copies, _ = pieces(i, odd)
        for side in range(3):
            copies(P1, side).start()

    planar(0, 0)

    def every(c, carry):
        for side in range(2):
            column(c, side).start()
        return carry


    def arrive(t, odd):
        z_copy(2 * t + odd, 0).wait_recv()
        planar(t, odd)

    def first(t, carry):
        pl.when(t > 0)(lambda: arrive(t, 0))
        arrive(t, 1)
        return carry

    def step(u, carry):
        @pl.when(u < 8)
        def _():
            for odd in range(2):
                _, copies, _ = pieces(u, odd)
                for side in range(3):
                    copies(P1, side, True).wait_recv()
                for side in range(3):
                    copies(P2, side).start()

        @pl.when(u < 4)
        def _():
            for odd in range(2):
                arrive(u + 4, odd)

        @pl.when(u == STRIPS_AT)
        def _():
            rows = e_ref.at[pl.ds(20 * core, RADIUS), centre, main]
            pltpu.make_async_copy(rows, rows, orecv.at[0]).wait()
            extra_beyond().wait_recv()
            for side in range(2):
                extra_column(OUTER, side).start()
                for m in range(2):
                    outer_column(m, side).start()

        @pl.when((u >= 2) & (u < 10))
        def _():
            for odd in range(2):
                b, copies, plane = pieces(u - 2, odd)
                for side in range(3):
                    copies(P2, side, True).wait_recv()
                plane().start()
                lay(b, core)

        @pl.when((u >= 3) & (u < 10))
        def _():
            for odd in range(2):
                b = 2 * (u - 3) + odd
                from_sibling(b).wait_recv()
                lay(b, 1 - core)

        @pl.when(u < 8)
        def _():
            build_rows(taps_ref, a_ref, u)

        @pl.when(u == INNER_AT)
        def _():
            own[1].wait()
            own[2].wait()
            for side in range(2):
                for c in range(2):
                    column(c, side).wait_recv()
                extra_column(OWN, side).wait_recv()
            inner_rows().start()
            inner_extra().start()

        @pl.when(u == 7)
        def _():
            inner_back = e_ref.at[pl.ds(20 - 20 * core, RADIUS), :, main]
            remote(inner_back, inner_back, xsend.at[5], xrecv.at[5], sibling).wait_recv()
            inner_extra().wait_recv()
            for q in range(RADIUS):
                top_lane = jnp.where(top, 7 - q, 16 + q)
                low_lane = jnp.where(bottom, 19 - q, 4 + q)
                spread(20 - 20 * core + q, INNER, jnp.where(core == 0, low_lane, top_lane))
            lax.fori_loop(RADIUS, RADIUS + 16, spread_own, 0)

        @pl.when((u >= 7) & (u < 10))
        def _():
            def early(k, c):
                n = 2 * (u - 7) + k
                for side in range(2):
                    column(n + 2, side).wait_recv()
                return features(n, c)

            lax.fori_loop(0, 2, early, 0)

        return carry

    lanes = lax.broadcasted_iota(jnp.int32, (SPAN, 128), 1)

    def spread(row, part, at):
        e_ref[row, :, MAIN:] = jnp.where(lanes == at, x_ref[part].astype(F32), 0.0).astype(BF)

    def spread_own(r, carry):
        spread(r, OWN, r)
        return carry

    def features(n, carry):
        stencil_rows(a_ref, e_ref, f_ref, jnp.where(core == 0, 7 - n, n))
        return carry

    def places(n, carry):
        i, odd, c = n // 4, (n // 2) % 2, n % 2
        place = jnp.where(odd == 1, z + 15 - i, z + i) % 16
        row = lax.broadcasted_iota(jnp.int32, (16, 512), 0)
        channel = lax.broadcasted_iota(jnp.int32, (16, 512), 1)
        at = (row >> 2) * 128 + (row & 3) * 8 + ((place // 8) * 64 + c * 32 + place % 8)
        perm_ref[pl.ds(pl.multiple_of(n * 16, 16), 16), :] = jnp.where(channel == at, 1.0, 0.0).astype(BF)
        return carry

    lax.fori_loop(0, 32, places, 0)

    lax.fori_loop(0, 2, first, 0)
    for q in range(RADIUS):
        strip(q).start()
    extra_beyond().start()
    for side in range(2):
        extra_column(OWN, side).start()
    lax.fori_loop(0, 8, every, 0)
    lax.fori_loop(2, 4, first, 0)
    lax.fori_loop(0, 10, step, 0)

    for side in range(2):
        for m in range(2):
            outer_column(m, side).wait_recv()
        extra_column(OUTER, side).wait_recv()
    for q in range(RADIUS):
        top_lane = jnp.where(top, 7 - q, 16 + q)
        low_lane = jnp.where(bottom, 19 - q, 4 + q)
        spread(20 * core + q, OUTER, jnp.where(core == 0, top_lane, low_lane))
    lax.fori_loop(6, 8, features, 0)

    def mix(n, carry):
        @pl.when(n == 1)
        def _():
            for b in (14, 15):
                from_sibling(b).wait_recv()
                lay(b, 1 - core)

        cols = pl.ds(pl.multiple_of(n * 256, 256), 256)
        total = lax.dot_general(
            f_ref[...], wt_ref[cols, :], (((1,), (1,)), ((), ())), preferred_element_type=F32
        )
        bias = lax.dot_general(
            bias_ref[...], perm_ref[cols, :].astype(F32), (((1,), (1,)), ((), ())),
            precision=lax.Precision.HIGHEST, preferred_element_type=F32,
        )
        total = total + bias
        value = 0.5 * total * (1.0 + lax.erf(total * math.sqrt(0.5)))
        value_ref[:, cols] = value.astype(BF)
        return carry

    lax.fori_loop(0, 2, mix, 0)
    out_ref[...] = jnp.dot(
        value_ref[...], perm_ref[...], preferred_element_type=F32
    ).astype(BF)

    def drain(i, carry):
        for odd in range(2):
            b, copies, plane = pieces(i, odd)

            @pl.when((i >= 0) if odd else (i > 0))
            def _():
                z_copy(b, 0).wait_send()

            for side in range(3):
                copies(P1, side).wait_send()
                copies(P2, side).wait_send()
            plane().wait_send()
        for side in range(2):
            column(i, side).wait_send()
        return carry

    lax.fori_loop(0, 8, drain, 0)
    for q in range(RADIUS):
        strip(q).wait_send()
    extra_beyond().wait_send()
    for side in range(2):
        for m in range(2):
            outer_column(m, side).wait_send()
        for part in (OWN, OUTER):
            extra_column(part, side).wait_send()
    inner_rows().wait_send()
    inner_extra().wait_send()


def body(latent, filters, widths, mix_weight, mix_bias):
    vmem = pl.BlockSpec(memory_space=pltpu.VMEM)
    dma = pltpu.SemaphoreType.DMA
    out = pl.pallas_call(
        main_kernel,
        out_shape=pltpu.VMEM((256, 512), BF),
        in_specs=[vmem] * 5,
        out_specs=vmem,
        scratch_shapes=[
            pltpu.VMEM((48, 128), BF),
            pltpu.VMEM((16, 128), BF),
            pltpu.VMEM((48, 128), F32),
            pltpu.VMEM((16, 2, 4, 4, 48, 128), BF),
            pltpu.VMEM((24, SPAN, MAIN + 128), BF),
            pltpu.VMEM((3, SPAN, 128), BF),
            pltpu.VMEM((BASES, 16, 2 * RADIUS + 1, 128), F32),
            pltpu.VMEM((8, 288, 512), BF),
            pltpu.VMEM((256, DEPTH), BF),
            pltpu.VMEM((512, DEPTH), BF),
            pltpu.VMEM((512, 512), BF),
            pltpu.VMEM((256, 512), BF),
            dma((4, 16, 3)),
            dma((4, 16, 3)),
            dma((10, 2)),
            dma((10, 2)),
            dma((7,)),
            dma((7,)),
            dma((RADIUS,)),
            dma((1,)),
            dma((3,)),
        ],
        compiler_params=pltpu.CompilerParams(
            collective_id=0, has_side_effects=True, vmem_limit_bytes=60 << 20
        ),
        name="sphere",
    )(
        jnp.transpose(mix_weight, (2, 0, 1)),
        latent,
        jnp.transpose(filters, (0, 2, 1, 3)),
        widths,
        mix_bias[None],
    )
    return out.reshape(16, 16, 512)


def solution(mesh):
    placed = (
        P("lat", "lon", None),
        P(None, "lat", None, None),
        P("lat", None),
        P(None, None, ("lat", "lon")),
        P(),
    )
    return jax.shard_map(
        body, mesh=mesh, in_specs=placed, out_specs=P("lat", "lon", None), check_vma=False
    )
```

```python
import math

import jax
import jax.numpy as jnp
from jax import lax
from jax.experimental import pallas as pl
from jax.experimental.pallas import tpu as pltpu
from jax.sharding import PartitionSpec as P

RADIUS = 4
REACH = 16
BASES = 9
MAIN = 640
SPAN = 48
DEPTH = 46 * 128
MESH = pl.DeviceIdType.MESH
BF = jnp.bfloat16
F32 = jnp.float32

Z1, P1, P2, DD = range(4)
OWN, OUTER, INNER = range(3)
STRIPS_AT = 6
INNER_AT = 5


def device_of(x, y, z, core):
    return (x * 4 + (z // 8) * 2 + core, y * 8 + z % 8)


def prepare(w_ref, latent, packed_ref, extra_ref, rows_ref):
    w = w_ref[0].astype(F32)
    for t in range(5):
        rows_ref[t * BASES : (t + 1) * BASES, :] = w[:, t * 128 : (t + 1) * 128]
    lane = lax.broadcasted_iota(jnp.int32, (BASES, 128), 1)
    row = lax.broadcasted_iota(jnp.int32, (BASES, 128), 0)
    last = jnp.where(lane == row, jnp.broadcast_to(w[:, MAIN:], (BASES, 128)), 0.0)
    rows_ref[45:46, :] = jnp.sum(last, axis=0, keepdims=True)
    rows_ref[46:48, :] = jnp.zeros((2, 128), F32)
    packed_ref[...] = rows_ref[...].astype(BF)
    lane = lax.broadcasted_iota(jnp.int32, (16, 128), 1)
    extra = jnp.zeros((16, 128), F32)
    for r in range(16):
        column = latent[r, :, MAIN:].astype(F32)
        extra = jnp.where(lane == RADIUS + r, jnp.broadcast_to(column, (16, 128)), extra)
    extra_ref[...] = extra.astype(BF)


def mask_taps(filters_ref, widths_ref, taps_ref):
    lane = lax.broadcasted_iota(jnp.int32, (16, 128), 1)
    inside = [
        jnp.abs(lane - REACH) <= jnp.broadcast_to(widths_ref[:, d : d + 1], (16, 128))
        for d in range(2 * RADIUS + 1)
    ]
    for k in range(BASES):
        taps = filters_ref[k].astype(F32)
        taps = jnp.pad(taps, ((0, 0), (0, 0), (0, 128 - taps.shape[2])))
        taps = jnp.stack([jnp.where(inside[d], taps[d], 0.0) for d in range(2 * RADIUS + 1)])
        taps_ref[k] = jnp.transpose(taps, (1, 0, 2))


def build_rows(taps_ref, a_ref, pair):
    lane = lax.broadcasted_iota(jnp.int32, (16, 128), 1)
    zero = jnp.zeros((16, 128), F32)
    for s in range(2):
        i = pair * 2 + s
        for k in range(BASES):
            taps = taps_ref[k, i]
            tiles = [None] * 4

            def put(t, part):
                tiles[t] = part if tiles[t] is None else tiles[t] + part

            for d in range(2 * RADIUS + 1):
                first, at = divmod(SPAN * (d + s), 128)
                line = jnp.broadcast_to(taps[d : d + 1], (16, 128))
                line = pltpu.roll(line, at, 1, stride=1, stride_axis=0)
                if at + SPAN > 128:
                    put(first, jnp.where(lane >= at, line, zero))
                    put(first + 1, jnp.where(lane < at, line, zero))
                else:
                    put(first, line)
            rows = pl.ds((s * BASES + k) * 16, 16)
            a_ref[pair, rows, :] = jnp.concatenate(tiles, 1).astype(BF)


def stencil_rows(a_ref, e_ref, f_ref, pair):
    lane = lax.broadcasted_iota(jnp.int32, (16, 128), 1)
    slab = e_ref[pl.ds(pair * 2, 10)].reshape(10 * SPAN, MAIN + 128)
    found = jnp.dot(a_ref[pair][:, : 10 * SPAN], slab, preferred_element_type=F32)
    for s in range(2):
        rows = pl.ds(pl.multiple_of((pair * 2 + s) * 16, 16), 16)
        last = jnp.zeros((16, 128), F32)
        for k in range(BASES):
            part = found[(s * BASES + k) * 16 : (s * BASES + k + 1) * 16]
            for t in range(5):
                h = t * BASES + k
                f_ref[rows, h * 128 : (h + 1) * 128] = part[:, t * 128 : (t + 1) * 128].astype(BF)
            tail = jnp.sum(part[:, MAIN:], axis=1, keepdims=True)
            last = jnp.where(lane == k, jnp.broadcast_to(tail, (16, 128)), last)
        f_ref[rows, 45 * 128 :] = last.astype(BF)


def main_kernel(
    w_ref, latent, filters_ref, widths_ref, bias_ref, out_ref,
    w_in, extra, rows_ref, g_ref, e_ref, x_ref, taps_ref, a_ref, f_ref, wt_ref, perm_ref, value_ref, shift_ref,
    send, recv, csend, crecv, xsend, xrecv, osend, orecv, own_sem,
):
    lat, lon = lax.axis_index("lat"), lax.axis_index("lon")
    x, core = lat // 4, lat % 2
    y = lon // 8
    z = ((lat // 2) % 2) * 8 + lon % 8
    xs = ((x + 3) % 4, (x + 1) % 4, (x + 2) % 4)
    ys = ((y + 3) % 4, (y + 1) % 4, (y + 2) % 4)
    to_x = [device_of(v, y, z, core) for v in xs]
    to_y = [device_of(x, v, z, core) for v in ys]
    to_z = [[device_of(x, y, (z + 16 + d * n) % 16, core) for d in (-1, 1)] for n in range(1, 9)]
    sibling = (lat + 1 - 2 * core, lon)
    to_lon = [(lat, (lon + 31) % 32), (lat, (lon + 1) % 32)]
    top, bottom = lat == 0, lat == 15
    pole = top | bottom
    beyond = (
        jnp.where(pole, lat, lat - 1 + 2 * core),
        jnp.where(pole, (lon + 16) % 32, lon),
    )

    barrier = pltpu.get_barrier_semaphore()
    peers = to_x + to_y + sum(to_z[:7], []) + to_z[7][:1] + [sibling] + to_lon + [beyond]
    for peer in peers:
        pl.semaphore_signal(barrier, inc=1, device_id=peer, device_id_type=MESH)
    prepare(w_ref, latent, w_in, extra, rows_ref)
    mask_taps(filters_ref, widths_ref, taps_ref)
    pl.semaphore_wait(barrier, len(peers))

    def remote(src, dst, s, r, where):
        return pltpu.make_async_remote_copy(
            src_ref=src, dst_ref=dst, send_sem=s, recv_sem=r,
            device_id=where, device_id_type=MESH,
        )

    main = pl.ds(0, MAIN)
    centre = pl.ds(16, 16)

    def column(c, side):
        n = jnp.where(core == 0, 7 - c, c)
        rows = pl.ds(RADIUS + 2 * n, 2)
        dst = e_ref.at[rows, pl.ds(32 * (1 - side), 16), main]
        return remote(
            latent.at[pl.ds(2 * n, 2), :, main], dst,
            csend.at[c, side], crecv.at[c, side], to_lon[side],
        )

    def outer_column(m, side):
        rows = pl.ds(20 * core + 2 * m, 2)
        dst = e_ref.at[rows, pl.ds(32 * (1 - side), 16), main]
        return remote(
            e_ref.at[rows, centre, main], dst,
            csend.at[8 + m, side], crecv.at[8 + m, side], to_lon[side],
        )

    def strip(q):
        row = jnp.where(pole, jnp.where(core == 0, 3 - q, 23 - q), jnp.where(core == 0, 20 + q, q))
        return remote(
            latent.at[12 * core + q, :, main], e_ref.at[row, centre, main],
            osend.at[q], orecv.at[0], beyond,
        )

    def extra_beyond():
        return remote(extra, x_ref.at[OUTER, centre, :], xsend.at[2], xrecv.at[2], beyond)

    def extra_column(part, side):
        src = extra if part == OWN else x_ref.at[OUTER, centre, :]
        dst = x_ref.at[part, pl.ds(32 * (1 - side), 16), :]
        return remote(src, dst, xsend.at[3 * part + side], xrecv.at[3 * part + side], to_lon[side])

    def inner_rows():
        src = e_ref.at[pl.ds(16 - 12 * core, RADIUS), :, main]
        dst = e_ref.at[pl.ds(20 * core, RADIUS), :, main]
        return remote(src, dst, xsend.at[5], xrecv.at[5], sibling)

    def inner_extra():
        return remote(x_ref.at[OWN], x_ref.at[INNER], xsend.at[6], xrecv.at[6], sibling)

    def block(b):
        return g_ref.at[b, core, x, y]

    def z_copy(b, side, hops=1):
        return remote(w_in, block(b), send.at[Z1, b, 0], recv.at[Z1, b, 0], to_z[hops - 1][side])

    for hops in range(1, 9):
        for side in range(2):
            if hops < 8 or side == 1:
                z_copy(2 * hops - side, side, hops).start()
    own = [
        pltpu.make_async_copy(w_in, block(0), own_sem.at[0]),
        pltpu.make_async_copy(
            latent.at[:, :, main], e_ref.at[pl.ds(RADIUS, 16), centre, main], own_sem.at[1]
        ),
        pltpu.make_async_copy(extra, x_ref.at[OWN, centre, :], own_sem.at[2]),
    ]
    for copy in own:
        copy.start()
    own[0].wait()

    def pieces(i, odd):
        b = 2 * i + odd
        near, far = (ys, xs) if odd else (xs, ys)
        to_near, to_far = (to_y, to_x) if odd else (to_x, to_y)
        me = (y, x) if odd else (x, y)

        def one(v):
            return g_ref.at[b, core, x, v] if odd else g_ref.at[b, core, v, y]

        def line(v):
            return g_ref.at[b, core, v] if odd else g_ref.at[b, core, :, v]

        def sem(stage, slot):
            return send.at[stage, b, slot], recv.at[stage, b, slot]

        def copies(stage, side, incoming=False):
            slot = (1, 0, 2)[side] if incoming else side
            if stage == P1:
                v = near[side] if incoming else me[0]
                return remote(one(v), one(v), *sem(P1, slot), to_near[side])
            v = far[side] if incoming else me[1]
            return remote(line(v), line(v), *sem(P2, slot), to_far[side])

        def plane():
            src = g_ref.at[b, core]
            return remote(src, src, send.at[DD, b, 0], recv.at[DD, b, 0], sibling)

        return b, copies, plane

    def from_sibling(b):
        dst = g_ref.at[b, 1 - core]
        return remote(dst, dst, send.at[DD, b, 0], recv.at[DD, b, 0], sibling)

    def lay(b, c):
        flat = g_ref[b, c].reshape(16, 48 * 128)
        wt_ref[pl.ds(pl.multiple_of((b * 2 + c) * 16, 16), 16), :] = flat[:, :DEPTH]

    def planar(i, odd):
        _, copies, _ = pieces(i, odd)
        for side in range(3):
            copies(P1, side).start()

    planar(0, 0)

    def every(c, carry):
        for side in range(2):
            column(c, side).start()
        return carry


    def arrive(t, odd):
        z_copy(2 * t + odd, 0).wait_recv()
        planar(t, odd)

    def first(t, carry):
        pl.when(t > 0)(lambda: arrive(t, 0))
        arrive(t, 1)
        return carry

    def step(u, carry):
        @pl.when(u < 8)
        def _():
            for odd in range(2):
                _, copies, _ = pieces(u, odd)
                for side in range(3):
                    copies(P1, side, True).wait_recv()
                for side in range(3):
                    copies(P2, side).start()

        @pl.when(u < 4)
        def _():
            for odd in range(2):
                arrive(u + 4, odd)

        @pl.when(u == STRIPS_AT)
        def _():
            rows = e_ref.at[pl.ds(20 * core, RADIUS), centre, main]
            pltpu.make_async_copy(rows, rows, orecv.at[0]).wait()
            extra_beyond().wait_recv()
            for side in range(2):
                extra_column(OUTER, side).start()
                for m in range(2):
                    outer_column(m, side).start()

        @pl.when((u >= 2) & (u < 10))
        def _():
            for odd in range(2):
                b, copies, plane = pieces(u - 2, odd)
                for side in range(3):
                    copies(P2, side, True).wait_recv()
                plane().start()
                lay(b, core)

        @pl.when((u >= 3) & (u < 10))
        def _():
            for odd in range(2):
                b = 2 * (u - 3) + odd
                from_sibling(b).wait_recv()
                lay(b, 1 - core)

        @pl.when(u < 8)
        def _():
            build_rows(taps_ref, a_ref, u)

        @pl.when(u == INNER_AT)
        def _():
            own[1].wait()
            own[2].wait()
            for side in range(2):
                for c in range(2):
                    column(c, side).wait_recv()
                extra_column(OWN, side).wait_recv()
            inner_rows().start()
            inner_extra().start()

        @pl.when(u == 7)
        def _():
            inner_back = e_ref.at[pl.ds(20 - 20 * core, RADIUS), :, main]
            remote(inner_back, inner_back, xsend.at[5], xrecv.at[5], sibling).wait_recv()
            inner_extra().wait_recv()
            for q in range(RADIUS):
                top_lane = jnp.where(top, 7 - q, 16 + q)
                low_lane = jnp.where(bottom, 19 - q, 4 + q)
                spread(20 - 20 * core + q, INNER, jnp.where(core == 0, low_lane, top_lane))
            lax.fori_loop(RADIUS, RADIUS + 16, spread_own, 0)

        @pl.when((u >= 7) & (u < 10))
        def _():
            def early(k, c):
                n = 2 * (u - 7) + k
                for side in range(2):
                    column(n + 2, side).wait_recv()
                return features(n, c)

            lax.fori_loop(0, 2, early, 0)

        return carry

    lanes = lax.broadcasted_iota(jnp.int32, (SPAN, 128), 1)

    def spread(row, part, at):
        e_ref[row, :, MAIN:] = jnp.where(lanes == at, x_ref[part].astype(F32), 0.0).astype(BF)

    def spread_own(r, carry):
        spread(r, OWN, r)
        return carry

    def features(n, carry):
        stencil_rows(a_ref, e_ref, f_ref, jnp.where(core == 0, 7 - n, n))
        return carry

    def places(n, carry):
        i, odd, c = n // 4, (n // 2) % 2, n % 2
        place = jnp.where(odd == 1, z + 15 - i, z + i) % 16
        row = lax.broadcasted_iota(jnp.int32, (16, 512), 0)
        channel = lax.broadcasted_iota(jnp.int32, (16, 512), 1)
        at = (row >> 2) * 128 + (row & 3) * 8 + ((place // 8) * 64 + c * 32 + place % 8)
        perm_ref[pl.ds(pl.multiple_of(n * 16, 16), 16), :] = jnp.where(channel == at, 1.0, 0.0).astype(BF)
        return carry

    lax.fori_loop(0, 32, places, 0)
    for n in range(2):
        cols = pl.ds(n * 256, 256)
        shift_ref[:, cols] = lax.dot_general(
            bias_ref[...], perm_ref[cols, :].astype(F32), (((1,), (1,)), ((), ())),
            precision=lax.Precision.HIGHEST, preferred_element_type=F32,
        )

    lax.fori_loop(0, 2, first, 0)
    for q in range(RADIUS):
        strip(q).start()
    extra_beyond().start()
    for side in range(2):
        extra_column(OWN, side).start()
    lax.fori_loop(0, 8, every, 0)
    lax.fori_loop(2, 4, first, 0)
    lax.fori_loop(0, 10, step, 0)

    for side in range(2):
        for m in range(2):
            outer_column(m, side).wait_recv()
        extra_column(OUTER, side).wait_recv()
    for q in range(RADIUS):
        top_lane = jnp.where(top, 7 - q, 16 + q)
        low_lane = jnp.where(bottom, 19 - q, 4 + q)
        spread(20 * core + q, OUTER, jnp.where(core == 0, top_lane, low_lane))
    lax.fori_loop(6, 8, features, 0)

    def mix(n, carry):
        @pl.when(n == 1)
        def _():
            for b in (14, 15):
                from_sibling(b).wait_recv()
                lay(b, 1 - core)

        cols = pl.ds(pl.multiple_of(n * 256, 256), 256)
        total = lax.dot_general(
            f_ref[...], wt_ref[cols, :], (((1,), (1,)), ((), ())), preferred_element_type=F32
        )
        total = total + shift_ref[:, cols]
        value = 0.5 * total * (1.0 + lax.erf(total * math.sqrt(0.5)))
        value_ref[:, cols] = value.astype(BF)
        return carry

    lax.fori_loop(0, 2, mix, 0)
    out_ref[...] = jnp.dot(
        value_ref[...], perm_ref[...], preferred_element_type=F32
    ).astype(BF)

    def drain(i, carry):
        for odd in range(2):
            b, copies, plane = pieces(i, odd)

            @pl.when((i >= 0) if odd else (i > 0))
            def _():
                z_copy(b, 0).wait_send()

            for side in range(3):
                copies(P1, side).wait_send()
                copies(P2, side).wait_send()
            plane().wait_send()
        for side in range(2):
            column(i, side).wait_send()
        return carry

    lax.fori_loop(0, 8, drain, 0)
    for q in range(RADIUS):
        strip(q).wait_send()
    extra_beyond().wait_send()
    for side in range(2):
        for m in range(2):
            outer_column(m, side).wait_send()
        for part in (OWN, OUTER):
            extra_column(part, side).wait_send()
    inner_rows().wait_send()
    inner_extra().wait_send()


def body(latent, filters, widths, mix_weight, mix_bias):
    vmem = pl.BlockSpec(memory_space=pltpu.VMEM)
    dma = pltpu.SemaphoreType.DMA
    out = pl.pallas_call(
        main_kernel,
        out_shape=pltpu.VMEM((256, 512), BF),
        in_specs=[vmem] * 5,
        out_specs=vmem,
        scratch_shapes=[
            pltpu.VMEM((48, 128), BF),
            pltpu.VMEM((16, 128), BF),
            pltpu.VMEM((48, 128), F32),
            pltpu.VMEM((16, 2, 4, 4, 48, 128), BF),
            pltpu.VMEM((24, SPAN, MAIN + 128), BF),
            pltpu.VMEM((3, SPAN, 128), BF),
            pltpu.VMEM((BASES, 16, 2 * RADIUS + 1, 128), F32),
            pltpu.VMEM((8, 288, 512), BF),
            pltpu.VMEM((256, DEPTH), BF),
            pltpu.VMEM((512, DEPTH), BF),
            pltpu.VMEM((512, 512), BF),
            pltpu.VMEM((256, 512), BF),
            pltpu.VMEM((1, 512), F32),
            dma((4, 16, 3)),
            dma((4, 16, 3)),
            dma((10, 2)),
            dma((10, 2)),
            dma((7,)),
            dma((7,)),
            dma((RADIUS,)),
            dma((1,)),
            dma((3,)),
        ],
        compiler_params=pltpu.CompilerParams(
            collective_id=0, has_side_effects=True, vmem_limit_bytes=60 << 20
        ),
        name="sphere",
    )(
        jnp.transpose(mix_weight, (2, 0, 1)),
        latent,
        jnp.transpose(filters, (0, 2, 1, 3)),
        widths,
        mix_bias[None],
    )
    return out.reshape(16, 16, 512)


def solution(mesh):
    placed = (
        P("lat", "lon", None),
        P(None, "lat", None, None),
        P("lat", None),
        P(None, None, ("lat", "lon")),
        P(),
    )
    return jax.shard_map(
        body, mesh=mesh, in_specs=placed, out_specs=P("lat", "lon", None), check_vma=False
    )
```
